256 devices in a mesh: aux: 16 (over z, core), occ: 4 (over y), vir: 4 (over x).
Axes of the slice: x: 4, y: 4, z: 8, core: 2. Of those that a mesh axis runs over, the one named last changes fastest.
Arguments:
- b_factors: bfloat16 [32, 3072, 8192], P('occ', 'vir', 'aux'), may hold values from -0.018310547 to 0.018310547
- right_side: float32 [32, 3072], P('occ', 'vir'), may hold values from -40 to 40
- occ_energy: float32 [32], P('occ'), may hold values from -3 to -0.5
- vir_energy: float32 [3072], P('vir'), may hold values from 0.5 to 6
Outputs:
- z_vector: float32 [32, 3072], P('occ', 'vir')
- residual: float32 [32, 3072], P('occ', 'vir')
The draws below stay inside these ranges and needn't reach their ends.
All inputs are finite; a program needn't handle non-finite values.
Results may differ from the reference program's by a relative error of at most 0.023.
Values may be sent and summed in bfloat16 or wider, within the bound.
A program may use at most 64 MiB of HBM per device.

```python
import math
import jax
import jax.numpy as jnp
from jax import lax

V = 3072
Q = 8192
ITERS = 3
OCC = 32


def draw_right_side(key, part):
    key_noise, key_rows, key_cols = jax.random.split(jax.random.fold_in(key, 71), 3)
    row_scale = jnp.linspace(1.0, 3.0, OCC) * jax.random.uniform(key_rows, (OCC,), jnp.float32, 0.6, 1.4)
    col_scale = jnp.linspace(1.0, 3.0, V) * jax.random.uniform(key_cols, (V,), jnp.float32, 0.6, 1.4)
    noise = jax.random.normal(key_noise, (OCC, V), jnp.float32)
    values = noise * row_scale[:, None] * col_scale[None, :] / 3.0
    return jnp.clip(values, -40.0, 40.0)


def levels(key, shape, pieces, low, high):
    def one(position, shards_of):
        heights = jax.random.uniform(jax.random.fold_in(jax.random.fold_in(key, 6), position), (shards_of,), jnp.float32, low / len(pieces), high / len(pieces))
        return jnp.repeat(jnp.exp(heights), shape[position] // shards_of).reshape((-1,) + (1,) * (len(shape) - position - 1))

    factor_of = one(*pieces[0])
    for cut in pieces[1:]:
        factor_of = factor_of * one(*cut)
    return factor_of


def gaussian(key, shape, deviation, limit, cuts=(), held_as=jnp.bfloat16):
    result = jax.random.normal(key, shape, jnp.float32) * deviation
    if len(cuts) > 0:
        result = levels(key, shape, cuts, -0.22, 0.18) * result
    return jnp.clip(result, min=-limit, max=limit).astype(held_as)


def setup_inputs(seed: int = 0) -> dict:
    keys = jax.random.split(jax.random.key(seed), 5)
    return {
        "b_factors": gaussian(keys[0], (OCC, V, Q), (1.0 / (OCC * V + Q) ** 0.5), 0.018310547, ((0, 4), (1, 4), (2, 16))),
        "right_side": draw_right_side(jax.random.fold_in(keys[4], 71), 0),
        "occ_energy": jnp.clip(-3.0 + 2.5 * jax.random.uniform(keys[2], (OCC,), jnp.float32) ** levels(keys[2], (OCC,), ((0, 4),), -0.2, 0.2), -3.0, -0.5),
        "vir_energy": jnp.clip(0.5 + 5.5 * jax.random.uniform(keys[3], (V,), jnp.float32) ** levels(keys[3], (V,), ((0, 4),), -0.2, 0.2), 0.5, 6.0),
    }


def respond(b_factors, trial, denom):
    trial_h = lax.optimization_barrier(trial.astype(jnp.bfloat16)).astype(jnp.float32)
    width = math.gcd(Q, 512)
    count = Q // width

    def block(index, carry):
        coulomb, exchange = carry
        start = (index * width).astype(jnp.int32)
        part = lax.dynamic_slice_in_dim(b_factors, start, width, 2).astype(jnp.float32)
        gamma = jnp.einsum('iaq,ia->q', part, trial_h, precision=lax.Precision.HIGHEST)
        gamma = lax.optimization_barrier(gamma.astype(jnp.bfloat16)).astype(jnp.float32)
        coulomb = coulomb + jnp.einsum('iaq,q->ia', part, gamma, precision=lax.Precision.HIGHEST)
        pairs = jnp.einsum('ibq,jb->ijq', part, trial_h, precision=lax.Precision.HIGHEST)
        pairs = lax.optimization_barrier(pairs.astype(jnp.bfloat16)).astype(jnp.float32)
        exchange = exchange + jnp.einsum('jaq,ijq->ia', part, pairs, precision=lax.Precision.HIGHEST)
        return coulomb, exchange

    empty = jnp.zeros(trial.shape, jnp.float32)
    coulomb, exchange = lax.fori_loop(0, count, block, (empty, empty))
    return denom * trial + 4.0 * coulomb - exchange


def reference(b_factors, right_side, occ_energy, vir_energy):
    denom = vir_energy[None, :] - occ_energy[:, None]
    z_vector = jnp.zeros_like(right_side)
    residual = right_side
    precond = residual / denom
    direction = precond
    rz_now = jnp.sum(residual * precond)
    for step in range(ITERS):
        image = respond(b_factors, direction, denom)
        alpha = rz_now / jnp.sum(direction * image)
        z_vector = z_vector + alpha * direction
        residual = residual - alpha * image
        precond = residual / denom
        rz_next = jnp.sum(residual * precond)
        direction = precond + (rz_next / rz_now) * direction
        rz_now = rz_next
    return z_vector, residual
```

```python
import functools

import jax
import jax.numpy as jnp
from jax import lax
from jax.experimental import pallas as pl
from jax.experimental.pallas import tpu as pltpu
from jax.sharding import PartitionSpec as P

ITERS = 3
MESH = pl.DeviceIdType.MESH
LANES = 128
ROWS = 8


def wait_bytes(ref, sem):
    pltpu.make_async_copy(ref, ref, sem).wait()


def kernel(
    sizes,
    b_hbm,
    right_ref,
    denom_ref,
    z_out,
    residual_out,
    b_ref,
    r_full,
    d_full,
    xh_ref,
    z_ref,
    x_ref,
    dir_ref,
    along_ref,
    p1_send,
    p1_recv,
    sums_ref,
    pairs_ref,
    gamma_ref,
    acc_ref,
    e_ref,
    rs_recv,
    total_ref,
    dots_ref,
    b_sem,
    init_sem,
    sems,
):
    n_aux, n_occ, n_vir = sizes
    aux, occ, vir = lax.axis_index("aux"), lax.axis_index("occ"), lax.axis_index("vir")
    n_i, n_a, n_p = b_ref.shape
    tiles = n_a // LANES
    n_all = n_occ * n_i
    plane, column = n_occ * n_vir, n_aux * n_occ
    quarter = n_p // n_vir
    owners = [(k * n_aux) // tiles for k in range(tiles)]

    def device(aux_at, occ_at, vir_at):
        return {"aux": aux_at, "occ": occ_at, "vir": vir_at}

    def send(src, dst, send_sem, recv_sem, where):
        pltpu.make_async_remote_copy(
            src_ref=src,
            dst_ref=dst,
            send_sem=send_sem,
            recv_sem=recv_sem,
            device_id=where,
            device_id_type=MESH,
        ).start()

    def plane_peer(step):
        return lax.rem(occ + step // n_vir, n_occ), lax.rem(vir + step % n_vir, n_vir)

    def column_peer(step):
        place = lax.rem(aux * n_occ + occ + step, column)
        return place // n_occ, lax.rem(place, n_occ)

    def load(i):
        return pltpu.make_async_copy(b_hbm.at[i], b_ref.at[i], b_sem.at[i])

    for i in range(n_i):
        load(i).start()

    barrier = pltpu.get_barrier_semaphore()

    @pl.loop(1, column)
    def _(step):
        aux_at, occ_at = column_peer(step)
        pl.semaphore_signal(barrier, inc=1, device_id=device(aux_at, occ_at, vir), device_id_type=MESH)

    for step in range(1, plane):
        if step % n_vir:
            occ_at, vir_at = plane_peer(step)
            pl.semaphore_signal(barrier, inc=1, device_id=device(aux, occ_at, vir_at), device_id_type=MESH)

    for k in range(tiles):
        cut = slice(k * LANES, (k + 1) * LANES)
        r_full[occ, k] = right_ref[:, cut]
        d_full[occ, k] = denom_ref[:, cut]

    pl.semaphore_wait(barrier, column - 1 + n_occ * (n_vir - 1))

    for step in range(1, n_occ):
        where = device(aux, lax.rem(occ + step, n_occ), vir)
        send(r_full.at[occ], r_full.at[occ], init_sem.at[0], init_sem.at[1], where)
        send(d_full.at[occ], d_full.at[occ], init_sem.at[2], init_sem.at[3], where)
    others = pl.ds(0, n_occ - 1)
    wait_bytes(r_full.at[others], init_sem.at[1])
    wait_bytes(d_full.at[others], init_sem.at[3])
    wait_bytes(r_full.at[others], init_sem.at[0])
    wait_bytes(d_full.at[others], init_sem.at[2])

    is_owner = functools.reduce(jnp.logical_or, [aux == owner for owner in owners])
    my_tile = occ * tiles + sum(jnp.where(aux == owner, k, 0) for k, owner in enumerate(owners))
    flat = (n_occ * tiles, ROWS, LANES)

    z_ref[...] = jnp.zeros_like(z_ref)
    rz_now = alpha = None

    for turn in range(ITERS):
        sem = functools.partial(lambda turn, index: sems.at[turn, index], turn)

        x = r_full[...] / d_full[...]
        x_ref[...] = x
        for o in range(0, n_occ, 2):
            for k in range(tiles):
                both = jnp.concatenate([x[o, k], x[o + 1, k]], axis=0)
                xh_ref[o * ROWS : (o + 2) * ROWS, k * LANES : (k + 1) * LANES] = both.astype(jnp.bfloat16)

        mine = p1_recv.at[turn, occ * n_vir + vir]
        xh = xh_ref[...]

        @pl.loop(0, n_i // 2)
        def _(half):
            i = half * 2
            if turn == 0:
                load(i).wait()
                load(i + 1).wait()
            one = jnp.dot(xh, b_ref[i], preferred_element_type=jnp.float32)
            two = jnp.dot(xh, b_ref[i + 1], preferred_element_type=jnp.float32)
            rows = pl.ds(pl.multiple_of(half * 2 * ROWS, 2 * ROWS), 2 * ROWS)
            for o in range(n_occ):
                for q in range(n_vir):
                    cut = (slice(o * ROWS, (o + 1) * ROWS), slice(q * quarter, (q + 1) * quarter))
                    both = jnp.concatenate([one[cut], two[cut]], axis=0).astype(jnp.bfloat16)
                    p1_send[turn, o * n_vir + q, rows, :] = both

        for step in range(1, plane):
            occ_at, vir_at = plane_peer(step)
            send(
                p1_send.at[turn, occ_at * n_vir + vir_at],
                p1_recv.at[turn, occ * n_vir + vir],
                sem(0),
                sem(1),
                device(aux, occ_at, vir_at),
            )
        mine[...] = p1_send[turn, occ * n_vir + vir]
        wait_bytes(p1_recv.at[turn, pl.ds(0, plane - 1)], sem(1))

        for o in range(n_occ):
            total = p1_recv[turn, o * n_vir].astype(jnp.float32)
            for v in range(1, n_vir):
                total = total + p1_recv[turn, o * n_vir + v].astype(jnp.float32)
            sums_ref[o * n_i * ROWS : (o + 1) * n_i * ROWS, :] = total
        for j in range(ROWS):
            column_j = sums_ref[pl.ds(j, n_all, stride=ROWS), :]
            pairs_ref[turn, vir, j * n_all : (j + 1) * n_all, :] = column_j.astype(jnp.bfloat16)
        for step in range(1, n_vir):
            send(
                pairs_ref.at[turn, vir],
                pairs_ref.at[turn, vir],
                sem(2),
                sem(3),
                device(aux, occ, lax.rem(vir + step, n_vir)),
            )
        diagonal = sums_ref[pl.ds(occ * n_i * ROWS, ROWS, stride=ROWS + 1), :]
        gamma_ref[turn, occ * n_vir + vir] = jnp.sum(diagonal, axis=0, keepdims=True)
        for step in range(1, plane):
            occ_at, vir_at = plane_peer(step)
            at = gamma_ref.at[turn, occ * n_vir + vir]
            send(at, at, sem(4), sem(5), device(aux, occ_at, vir_at))

        wait_bytes(pairs_ref.at[turn, pl.ds(0, n_vir - 1)], sem(3))
        wait_bytes(gamma_ref.at[turn, pl.ds(0, plane - 1)], sem(5))
        gamma = []
        for q in range(n_vir):
            parts = [gamma_ref[turn, o * n_vir + q] for o in range(n_occ)]
            gamma.append(functools.reduce(jnp.add, parts))
        gamma = jnp.concatenate(gamma, axis=1)
        gamma = jnp.broadcast_to(gamma, (2 * ROWS, n_p))
        row = lax.broadcasted_iota(jnp.int32, (2 * ROWS, n_p), 0)
        acc_ref[...] = jnp.zeros_like(acc_ref)

        @pl.loop(0, ROWS)
        def _(j):
            rows = pl.ds(pl.multiple_of(j * n_all, n_all), n_all)
            left = jnp.concatenate([pairs_ref[turn, q, rows, :] for q in range(n_vir)], axis=1)
            below = jnp.where(row == j, gamma, 0.0).astype(jnp.bfloat16)
            left = jnp.concatenate([left, below], axis=0)
            acc_ref[...] += lax.dot_general(
                left, b_ref[j], (((1,), (1,)), ((), ())), preferred_element_type=jnp.float32
            )

        for o in range(n_occ):
            for k in range(tiles):
                cut = (slice(o * ROWS, (o + 1) * ROWS), slice(k * LANES, (k + 1) * LANES))
                e_ref[turn, o * tiles + k] = -acc_ref[cut]
        for k in range(tiles):
            coulomb = acc_ref[n_all : n_all + ROWS, k * LANES : (k + 1) * LANES]
            e_ref[turn, occ * tiles + k] += 4.0 * coulomb

        place = aux * n_occ + occ
        for o in range(n_occ):
            for k in range(tiles):
                here = jnp.logical_and(occ == o, aux == owners[k])

                @pl.when(jnp.logical_not(here))
                def _():
                    send(
                        e_ref.at[turn, o * tiles + k],
                        rs_recv.at[turn, place],
                        sem(6),
                        sem(7),
                        device(owners[k], o, vir),
                    )

        n_tiles = n_occ * tiles

        @pl.when(is_owner)
        def _():
            rs_recv[turn, place] = e_ref[turn, my_tile]
            wait_bytes(rs_recv.at[turn, pl.ds(0, column - 1)], sem(7))
            parts = [jnp.zeros((ROWS, LANES), jnp.float32) for _ in range(4)]
            for source in range(column):
                parts[source % 4] = parts[source % 4] + rs_recv[turn, source]
            total_ref[turn, my_tile] = (parts[0] + parts[1]) + (parts[2] + parts[3])

            @pl.loop(1, column)
            def _(step):
                aux_at, occ_at = column_peer(step)
                at = total_ref.at[turn, my_tile]
                send(at, at, sem(8), sem(9), device(aux_at, occ_at, vir))

            wait_bytes(total_ref.at[turn, pl.ds(0, n_tiles - 1)], sem(9))

        @pl.when(jnp.logical_not(is_owner))
        def _():
            wait_bytes(total_ref.at[turn], sem(9))

        x = x_ref[...].reshape(flat)
        image = d_full[...].reshape(flat) * x + total_ref[turn]
        dots_ref[turn, vir, 0] = jnp.sum(r_full[...].reshape(flat) * x, axis=0)
        dots_ref[turn, vir, 1] = jnp.sum(x * image, axis=0)
        for step in range(1, n_vir):
            at = dots_ref.at[turn, vir]
            send(at, at, sem(10), sem(11), device(aux, occ, lax.rem(vir + step, n_vir)))
        wait_bytes(dots_ref.at[turn, pl.ds(0, n_vir - 1)], sem(11))
        dots = functools.reduce(jnp.add, [dots_ref[turn, v] for v in range(n_vir)])
        rz_next = jnp.sum(dots[0], keepdims=True)
        product = jnp.sum(dots[1], keepdims=True)

        if turn == 0:
            alpha = rz_next / product
            direction, along = x, image
        else:
            ratio = rz_next / rz_now
            alpha = rz_next / (product - ratio * rz_next / alpha)
            direction = x + ratio[None] * dir_ref[...].reshape(flat)
            along = image + ratio[None] * along_ref[...].reshape(flat)
        rz_now = rz_next
        shape = r_full.shape
        if turn + 1 < ITERS:
            dir_ref[...] = direction.reshape(shape)
            along_ref[...] = along.reshape(shape)
        z_ref[...] += (alpha[None] * direction).reshape(shape)
        r_full[...] -= (alpha[None] * along).reshape(shape)

    for k in range(tiles):
        cut = slice(k * LANES, (k + 1) * LANES)
        z_out[:, cut] = z_ref[occ, k]
        residual_out[:, cut] = r_full[occ, k]

    n_tiles = n_occ * tiles
    for turn in range(ITERS):
        wait_bytes(p1_send.at[turn, pl.ds(0, plane - 1)], sems.at[turn, 0])
        wait_bytes(pairs_ref.at[turn, pl.ds(0, n_vir - 1)], sems.at[turn, 2])
        wait_bytes(gamma_ref.at[turn, pl.ds(0, plane - 1)], sems.at[turn, 4])
        wait_bytes(dots_ref.at[turn, pl.ds(0, n_vir - 1)], sems.at[turn, 10])

    @pl.when(is_owner)
    def _():
        for turn in range(ITERS):
            wait_bytes(e_ref.at[turn, pl.ds(0, n_tiles - 1)], sems.at[turn, 6])
            wait_bytes(rs_recv.at[turn, pl.ds(0, column - 1)], sems.at[turn, 8])

    @pl.when(jnp.logical_not(is_owner))
    def _():
        for turn in range(ITERS):
            wait_bytes(e_ref.at[turn], sems.at[turn, 6])


def solution(mesh):
    sizes = tuple(mesh.shape[name] for name in ("aux", "occ", "vir"))
    n_aux, n_occ, n_vir = sizes

    def shards(b_factors, right_side, occ_energy, vir_energy):
        n_i, n_a, n_p = b_factors.shape
        tiles = n_a // LANES
        plane, column = n_occ * n_vir, n_aux * n_occ
        n_all = n_occ * n_i
        denom = vir_energy[None, :] - occ_energy[:, None]
        f32, bf16 = jnp.float32, jnp.bfloat16
        whole = pltpu.VMEM((n_occ, tiles, ROWS, LANES), f32)
        vmem = pl.BlockSpec(memory_space=pltpu.VMEM)
        return tuple(
            pl.pallas_call(
                functools.partial(kernel, sizes),
                out_shape=[jax.ShapeDtypeStruct((n_i, n_a), f32)] * 2,
                in_specs=[pl.BlockSpec(memory_space=pl.ANY), vmem, vmem],
                out_specs=[vmem, vmem],
                scratch_shapes=[
                    pltpu.VMEM((n_i, n_a, n_p), bf16),
                    whole,
                    whole,
                    pltpu.VMEM((n_all, n_a), bf16),
                    whole,
                    whole,
                    whole,
                    whole,
                    pltpu.VMEM((ITERS, plane, n_i * ROWS, LANES), bf16),
                    pltpu.VMEM((ITERS, plane, n_i * ROWS, LANES), bf16),
                    pltpu.VMEM((n_all * ROWS, LANES), f32),
                    pltpu.VMEM((ITERS, n_vir, n_all * ROWS, LANES), bf16),
                    pltpu.VMEM((ITERS, plane, 1, LANES), f32),
                    pltpu.VMEM((n_all + 2 * ROWS, n_a), f32),
                    pltpu.VMEM((ITERS, n_occ * tiles, ROWS, LANES), f32),
                    pltpu.VMEM((ITERS, column, ROWS, LANES), f32),
                    pltpu.VMEM((ITERS, n_occ * tiles, ROWS, LANES), f32),
                    pltpu.VMEM((ITERS, n_vir, 2, ROWS, LANES), f32),
                    pltpu.SemaphoreType.DMA((n_i,)),
                    pltpu.SemaphoreType.DMA((4,)),
                    pltpu.SemaphoreType.DMA((ITERS, 12)),
                ],
                compiler_params=pltpu.CompilerParams(
                    collective_id=0, has_side_effects=True, vmem_limit_bytes=60 * 2**20
                ),
            )(b_factors, right_side, denom)
        )

    in_specs = (P("occ", "vir", "aux"), P("occ", "vir"), P("occ"), P("vir"))
    out_specs = (P("occ", "vir"), P("occ", "vir"))
    return jax.shard_map(shards, mesh=mesh, in_specs=in_specs, out_specs=out_specs, check_vma=False)
```

```python
import functools

import jax
import jax.numpy as jnp
from jax import lax
from jax.experimental import pallas as pl
from jax.experimental.pallas import tpu as pltpu
from jax.sharding import PartitionSpec as P

ITERS = 3
MESH = pl.DeviceIdType.MESH
LANES = 128
ROWS = 8


def wait_bytes(ref, sem):
    pltpu.make_async_copy(ref, ref, sem).wait()


def kernel(
    sizes,
    b_hbm,
    right_hbm,
    occ_smem,
    vir_hbm,
    both_out,
    b_ref,
    right_ref,
    vir_ref,
    rd_ref,
    xh_ref,
    z_ref,
    x_ref,
    dir_ref,
    along_ref,
    p1_send,
    p1_recv,
    sums_ref,
    pairs_ref,
    diag_ref,
    gamma_ref,
    acc_ref,
    a_send,
    a_recv,
    b_recv,
    total_ref,
    da_recv,
    db_recv,
    dc_recv,
    b_sem,
    in_sem,
    sems,
):
    n_aux, n_occ, n_vir = sizes
    aux, occ, vir = lax.axis_index("aux"), lax.axis_index("occ"), lax.axis_index("vir")
    n_i, n_a, n_p = b_ref.shape
    tiles = n_a // LANES
    n_all = n_occ * n_i
    n_z, group = n_aux // 2, n_occ * 2
    per = tiles // 2
    z, core = aux // 2, lax.rem(aux, 2)
    plane = n_occ * n_vir
    quarter = n_p // n_vir
    here = occ * n_vir + vir
    spot = occ * 2 + core

    def device(aux_at, occ_at, vir_at):
        return {"aux": aux_at, "occ": occ_at, "vir": vir_at}

    def send(src, dst, send_sem, recv_sem, where):
        pltpu.make_async_remote_copy(
            src_ref=src,
            dst_ref=dst,
            send_sem=send_sem,
            recv_sem=recv_sem,
            device_id=where,
            device_id_type=MESH,
        ).start()

    def shifted(at, step, size):
        return lax.rem(at + step, size) if step else at

    def plane_peer(step):
        occ_at, vir_at = shifted(occ, step // n_vir, n_occ), shifted(vir, step % n_vir, n_vir)
        return occ_at * n_vir + vir_at, device(aux, occ_at, vir_at)

    def group_peer(step):
        occ_at, core_at = shifted(occ, step // 2, n_occ), shifted(core, step % 2, 2)
        return occ_at * 2 + core_at, device(z * 2 + core_at, occ_at, vir)

    def z_peer(step):
        return device(shifted(z, step, n_z) * 2 + core, occ, vir)

    def vir_peer(step):
        return device(aux, occ, shifted(vir, step, n_vir))

    def load(i):
        return pltpu.make_async_copy(b_hbm.at[i], b_ref.at[i], b_sem.at[i])

    inputs = [
        pltpu.make_async_copy(right_hbm, right_ref, in_sem.at[0]),
        pltpu.make_async_copy(vir_hbm, vir_ref, in_sem.at[1]),
    ]
    for copy in inputs:
        copy.start()
    for i in range(n_i):
        load(i).start()

    barrier = pltpu.get_barrier_semaphore()
    peers = [plane_peer(step)[1] for step in range(1, plane)]
    peers += [group_peer(step)[1] for step in range(1, group) if step % 2]
    peers += [z_peer(step) for step in range(1, n_z)]
    for peer in peers:
        pl.semaphore_signal(barrier, inc=1, device_id=peer, device_id_type=MESH)

    for copy in inputs:
        copy.wait()
    row = lax.broadcasted_iota(jnp.int32, (ROWS, LANES), 0)
    occ_tile = jnp.zeros((ROWS, LANES), jnp.float32)
    for i in range(ROWS):
        occ_tile = jnp.where(row == i, occ_smem[i], occ_tile)
    for k in range(tiles):
        cut = slice(k * LANES, (k + 1) * LANES)
        rd_ref[occ, 0, k] = right_ref[:, cut]
        rd_ref[occ, 1, k] = vir_ref[:, cut] - occ_tile

    pl.semaphore_wait(barrier, len(peers))

    for step in range(1, n_occ):
        at = rd_ref.at[occ]
        send(at, at, in_sem.at[2], in_sem.at[3], device(aux, shifted(occ, step, n_occ), vir))
    wait_bytes(rd_ref.at[pl.ds(0, n_occ - 1)], in_sem.at[3])

    z_ref[...] = jnp.zeros_like(z_ref)
    rz_now = alpha = None
    order = [0, 1] + [n_vir - 1 - step for step in range(n_vir - 2)]

    for turn in range(ITERS):
        sem = functools.partial(lambda turn, index: sems.at[turn, index], turn)

        x = rd_ref[:, 0] / rd_ref[:, 1]
        x_ref[...] = x
        for o in range(0, n_occ, 2):
            for k in range(tiles):
                both = jnp.concatenate([x[o, k], x[o + 1, k]], axis=0)
                xh_ref[o * ROWS : (o + 2) * ROWS, k * LANES : (k + 1) * LANES] = both.astype(jnp.bfloat16)

        xh = xh_ref[...]
        diag = jnp.zeros((ROWS, n_p), jnp.float32)
        wide = lax.broadcasted_iota(jnp.int32, (ROWS, n_p), 0)
        for i in range(0, n_i, 2):
            if turn == 0:
                load(i).wait()
                load(i + 1).wait()
            one = jnp.dot(xh, b_ref[i], preferred_element_type=jnp.float32)
            two = jnp.dot(xh, b_ref[i + 1], preferred_element_type=jnp.float32)
            for o in range(n_occ):
                rows = slice(o * ROWS, (o + 1) * ROWS)
                mine = wide + (occ - o) * n_all
                diag = diag + jnp.where(mine == i, one[rows], 0.0) + jnp.where(mine == i + 1, two[rows], 0.0)
                for q in range(n_vir):
                    cut = (rows, slice(q * quarter, (q + 1) * quarter))
                    both = jnp.concatenate([one[cut], two[cut]], axis=0).astype(jnp.bfloat16)
                    p1_send[turn, o * n_vir + q, i * ROWS : (i + 2) * ROWS, :] = both

        for step in range(1, plane):
            at, where = plane_peer(step)
            send(p1_send.at[turn, at], p1_recv.at[turn, here], sem(0), sem(1), where)
        gamma_ref[turn, here] = jnp.sum(diag, axis=0, keepdims=True)
        for step in range(1, plane):
            at = gamma_ref.at[turn, here]
            send(at, at, sem(2), sem(3), plane_peer(step)[1])
        p1_recv[turn, here] = p1_send[turn, here]
        wait_bytes(p1_recv.at[turn, pl.ds(0, plane - 1)], sem(1))

        for o in range(n_occ):
            total = p1_recv[turn, o * n_vir].astype(jnp.float32)
            for v in range(1, n_vir):
                total = total + p1_recv[turn, o * n_vir + v].astype(jnp.float32)
            sums_ref[o * n_i * ROWS : (o + 1) * n_i * ROWS, :] = total
        for j in range(ROWS):
            column_j = sums_ref[pl.ds(j, n_all, stride=ROWS), :]
            pairs_ref[turn, vir, j * n_all : (j + 1) * n_all, :] = column_j.astype(jnp.bfloat16)
        for step in range(1, n_vir):
            at = pairs_ref.at[turn, vir]
            send(at, at, sem(4), sem(16 + step), vir_peer(step))

        wait_bytes(gamma_ref.at[turn, pl.ds(0, plane - 1)], sem(3))
        gamma = functools.reduce(jnp.add, [gamma_ref[turn, s] for s in range(plane)])
        diag_ref[...] = gamma
        acc_ref[...] = jnp.zeros_like(acc_ref)
        tall = lax.broadcasted_iota(jnp.int32, (2 * ROWS, 2 * quarter), 0)

        for first in range(0, n_vir, 2):
            quarters = []
            for step in order[first : first + 2]:
                q = lax.rem(vir + n_vir - step, n_vir) if step else vir
                if step:
                    wait_bytes(pairs_ref.at[turn, q], sem(16 + step))
                quarters.append((q, pl.ds(pl.multiple_of(q * quarter, quarter), quarter)))
            gamma = jnp.concatenate([diag_ref[:, lanes] for _, lanes in quarters], axis=1)
            gamma = jnp.broadcast_to(gamma, tall.shape)
            total = acc_ref[...]
            for j in range(ROWS):
                rows = slice(j * n_all, (j + 1) * n_all)
                left = jnp.concatenate([pairs_ref[turn, q, rows, :] for q, _ in quarters], axis=1)
                below = jnp.where(tall == j, gamma, 0.0).astype(jnp.bfloat16)
                left = jnp.concatenate([left, below], axis=0)
                right = jnp.concatenate([b_ref[j, :, lanes] for _, lanes in quarters], axis=1)
                total = total + lax.dot_general(
                    left, right, (((1,), (1,)), ((), ())), preferred_element_type=jnp.float32
                )
            acc_ref[...] = total

        delta = jnp.zeros((ROWS, LANES), jnp.float32)
        for o in range(n_occ):
            scale = jnp.where(occ == o, 4.0, 0.0)
            for k in range(tiles):
                lanes = slice(k * LANES, (k + 1) * LANES)
                tile = scale * acc_ref[n_all : n_all + ROWS, lanes] - acc_ref[o * ROWS : (o + 1) * ROWS, lanes]
                a_send[turn, o * 2 + k // per, k % per] = tile
                delta = delta + tile * x_ref[o, k]
        for step in range(1, group):
            at, where = group_peer(step)
            send(a_send.at[turn, at], a_recv.at[turn, spot], sem(5), sem(6), where)
        da_recv[turn, spot] = jnp.sum(delta, axis=0, keepdims=True)
        for step in range(1, group):
            at = da_recv.at[turn, spot]
            send(at, at, sem(7), sem(8), group_peer(step)[1])
        a_recv[turn, spot] = a_send[turn, spot]
        r, d = rd_ref[:, 0], rd_ref[:, 1]
        flat = (n_occ * tiles, ROWS, LANES)
        rz_part = jnp.sum(jnp.sum((r * x_ref[...]).reshape(flat), axis=0), axis=0, keepdims=True)
        own = jnp.sum(jnp.sum((d * x_ref[...] * x_ref[...]).reshape(flat), axis=0), axis=0, keepdims=True)
        wait_bytes(a_recv.at[turn, pl.ds(0, group - 1)], sem(6))
        b_recv[turn, z] = functools.reduce(jnp.add, [a_recv[turn, s] for s in range(group)])
        for step in range(1, n_z):
            at = b_recv.at[turn, z]
            send(at, at, sem(9), sem(10), z_peer(step))
        wait_bytes(da_recv.at[turn, pl.ds(0, group - 1)], sem(8))
        db_recv[turn, z] = functools.reduce(jnp.add, [da_recv[turn, s] for s in range(group)])
        for step in range(1, n_z):
            at = db_recv.at[turn, z]
            send(at, at, sem(11), sem(12), z_peer(step))

        wait_bytes(b_recv.at[turn, pl.ds(0, n_z - 1)], sem(10))
        total_ref[turn, spot] = functools.reduce(jnp.add, [b_recv[turn, s] for s in range(n_z)])
        for step in range(1, group):
            at = total_ref.at[turn, spot]
            send(at, at, sem(13), sem(14), group_peer(step)[1])
        wait_bytes(db_recv.at[turn, pl.ds(0, n_z - 1)], sem(12))
        delta = functools.reduce(jnp.add, [db_recv[turn, s] for s in range(n_z)]) + own
        dc_recv[turn, vir] = jnp.concatenate([rz_part, delta], axis=0)
        for step in range(1, n_vir):
            at = dc_recv.at[turn, vir]
            send(at, at, sem(15), sem(16), vir_peer(step))
        wait_bytes(dc_recv.at[turn, pl.ds(0, n_vir - 1)], sem(16))
        dots = functools.reduce(jnp.add, [dc_recv[turn, v] for v in range(n_vir)])
        rz_next = jnp.sum(dots[0:1], axis=1, keepdims=True)
        product = jnp.sum(dots[1:2], axis=1, keepdims=True)
        if turn == 0:
            alpha = rz_next / product
        else:
            ratio = rz_next / rz_now
            alpha = rz_next / (product - ratio * rz_next / alpha)
        rz_now = rz_next

        wait_bytes(total_ref.at[turn, pl.ds(0, group - 1)], sem(14))
        if turn + 1 < ITERS:
            x = x_ref[...]
            image = rd_ref[:, 1] * x + total_ref[turn].reshape(x.shape)
            if turn == 0:
                wait_bytes(rd_ref.at[pl.ds(0, n_occ - 1)], in_sem.at[2])
                direction, along = x, image
            else:
                direction = x + ratio[None, None] * dir_ref[...]
                along = image + ratio[None, None] * along_ref[...]
            dir_ref[...] = direction
            along_ref[...] = along
            z_ref[...] += alpha[None, None] * direction
            rd_ref[:, 0] = rd_ref[:, 0] - alpha[None, None] * along
        else:
            for k in range(tiles):
                cut = slice(k * LANES, (k + 1) * LANES)
                x = x_ref[occ, k]
                image = rd_ref[occ, 1, k] * x + total_ref[turn, occ * 2 + k // per, k % per]
                both_out[0, :, cut] = z_ref[occ, k] + alpha * (x + ratio * dir_ref[occ, k])
                both_out[1, :, cut] = rd_ref[occ, 0, k] - alpha * (image + ratio * along_ref[occ, k])

    for turn in range(ITERS):
        wait_bytes(p1_send.at[turn, pl.ds(0, plane - 1)], sems.at[turn, 0])
        wait_bytes(gamma_ref.at[turn, pl.ds(0, plane - 1)], sems.at[turn, 2])
        wait_bytes(pairs_ref.at[turn, pl.ds(0, n_vir - 1)], sems.at[turn, 4])
        wait_bytes(a_send.at[turn, pl.ds(0, group - 1)], sems.at[turn, 5])
        wait_bytes(da_recv.at[turn, pl.ds(0, group - 1)], sems.at[turn, 7])
        wait_bytes(b_recv.at[turn, pl.ds(0, n_z - 1)], sems.at[turn, 9])
        wait_bytes(db_recv.at[turn, pl.ds(0, n_z - 1)], sems.at[turn, 11])
        wait_bytes(total_ref.at[turn, pl.ds(0, group - 1)], sems.at[turn, 13])
        wait_bytes(dc_recv.at[turn, pl.ds(0, n_vir - 1)], sems.at[turn, 15])


def solution(mesh):
    sizes = tuple(mesh.shape[name] for name in ("aux", "occ", "vir"))
    n_aux, n_occ, n_vir = sizes

    def shards(b_factors, right_side, occ_energy, vir_energy):
        n_i, n_a, n_p = b_factors.shape
        tiles = n_a // LANES
        plane, group, n_z = n_occ * n_vir, n_occ * 2, n_aux // 2
        n_all = n_occ * n_i
        f32, bf16 = jnp.float32, jnp.bfloat16
        whole = pltpu.VMEM((n_occ, tiles, ROWS, LANES), f32)
        anywhere = pl.BlockSpec(memory_space=pl.ANY)
        both = pl.pallas_call(
            functools.partial(kernel, sizes),
            out_shape=jax.ShapeDtypeStruct((2, n_i, n_a), f32),
            in_specs=[anywhere, anywhere, pl.BlockSpec(memory_space=pltpu.SMEM), anywhere],
            out_specs=pl.BlockSpec(memory_space=pltpu.VMEM),
            scratch_shapes=[
                pltpu.VMEM((n_i, n_a, n_p), bf16),
                pltpu.VMEM((n_i, n_a), f32),
                pltpu.VMEM((1, n_a), f32),
                pltpu.VMEM((n_occ, 2, tiles, ROWS, LANES), f32),
                pltpu.VMEM((n_all, n_a), bf16),
                whole,
                whole,
                whole,
                whole,
                pltpu.VMEM((ITERS, plane, n_i * ROWS, LANES), bf16),
                pltpu.VMEM((ITERS, plane, n_i * ROWS, LANES), bf16),
                pltpu.VMEM((n_all * ROWS, LANES), f32),
                pltpu.VMEM((ITERS, n_vir, n_all * ROWS, LANES), bf16),
                pltpu.VMEM((1, n_p), f32),
                pltpu.VMEM((ITERS, plane, 1, n_p), f32),
                pltpu.VMEM((n_all + 2 * ROWS, n_a), f32),
                pltpu.VMEM((ITERS, group, tiles // 2, ROWS, LANES), f32),
                pltpu.VMEM((ITERS, group, tiles // 2, ROWS, LANES), f32),
                pltpu.VMEM((ITERS, n_z, tiles // 2, ROWS, LANES), f32),
                pltpu.VMEM((ITERS, group, tiles // 2, ROWS, LANES), f32),
                pltpu.VMEM((ITERS, group, 1, LANES), f32),
                pltpu.VMEM((ITERS, n_z, 1, LANES), f32),
                pltpu.VMEM((ITERS, n_vir, 2, LANES), f32),
                pltpu.SemaphoreType.DMA((n_i,)),
                pltpu.SemaphoreType.DMA((4,)),
                pltpu.SemaphoreType.DMA((ITERS, 16 + n_vir)),
            ],
            compiler_params=pltpu.CompilerParams(
                collective_id=0, has_side_effects=True, vmem_limit_bytes=60 * 2**20
            ),
        )(b_factors, right_side, occ_energy, vir_energy.reshape(1, n_a))
        return both[0], both[1]

    in_specs = (P("occ", "vir", "aux"), P("occ", "vir"), P("occ"), P("vir"))
    out_specs = (P("occ", "vir"), P("occ", "vir"))
    return jax.shard_map(shards, mesh=mesh, in_specs=in_specs, out_specs=out_specs, check_vma=False)
```
